512 devices in a mesh: gx: 32 (over x, z), gy: 16 (over y, core).
Axes of the slice: x: 4, y: 8, z: 8, core: 2. Of those that a mesh axis runs over, the one named last changes fastest.
Arguments:
- right_side: float32 [2, 1024, 16384], P(None, 'gy', 'gx'), may hold values from -1.5 to 1.5
- faces: float32 [1024], P('gy'), may hold values from 0.149 to 6.69
- widths: float32 [1024], P('gy'), may hold values from 0.149 to 6.69
Outputs:
- pressure: float32 [2, 1024, 16384], P(None, 'gy', 'gx')
The draws below stay inside these ranges and needn't reach their ends.
All inputs are finite; a program needn't handle non-finite values.
Results may differ from the reference program's by a relative error of at most 0.00045.
Values sent between devices are 32-bit elements; how exact they have to be, the bound alone decides.
A program may use at most 64 MiB of HBM per device.

```python
import math
import jax
import jax.numpy as jnp
from jax import lax

NX = 16384
NY = 1024
ASPECT = 128
LEV = 2


def draw_right_side(key, part):
    key_list = jax.random.split(jax.random.fold_in(key, 5), 6)
    full_shape = (LEV, NY, NX)
    noise_part = 0.25 * jax.random.normal(key_list[0], full_shape, jnp.float32)
    stretch = jax.random.randint(key_list[1], (), NX // 48, NX // 24)
    offset = jax.random.randint(key_list[2], (), 0, NX // 24)
    columns = jnp.arange(NX, dtype=jnp.int32)
    block_index = jnp.minimum((columns + offset) // stretch, 63)
    magnitude = jax.random.uniform(key_list[3], (LEV, 64), jnp.float32, 0.75, 0.95)
    sign_flip = (2 * jax.random.randint(key_list[4], (LEV, 1), 0, 2) - 1).astype(jnp.float32)
    parity = 1.0 - 2.0 * (jnp.arange(64, dtype=jnp.int32) % 2).astype(jnp.float32)
    level_table = magnitude * parity[None, :] * sign_flip
    level_row = jnp.take(level_table, block_index, axis=1)
    phase_shift = jax.random.uniform(key_list[5], (LEV, 1), jnp.float32, 0.0, 2.0 * math.pi)
    row_index = jnp.arange(NY, dtype=jnp.float32)[None, :]
    profile = 0.8 + 0.2 * jnp.cos(2.0 * math.pi * row_index / NY + phase_shift)
    summed = noise_part + profile[:, :, None] * level_row[:, None, :]
    return jnp.clip(summed, -1.5, 1.5)


def wall_profile(key, salt_value):
    key_list = jax.random.split(jax.random.fold_in(key, salt_value), 2)
    wall_grade = jax.random.uniform(key_list[0], (), jnp.float32, -1.2, 1.2)
    row_index = jnp.arange(NY, dtype=jnp.float32)
    rough_part = jax.random.uniform(key_list[1], (NY,), jnp.float32, -0.7, 0.7)
    return jnp.exp(wall_grade * jnp.exp(-row_index / ASPECT) + rough_part)


def draw_faces(key, part):
    return wall_profile(key, 11)


def draw_widths(key, part):
    return wall_profile(key, 23)


def setup_inputs(seed: int = 0) -> dict:
    arg_keys = jax.random.split(jax.random.key(seed), 4)
    return {
        "right_side": draw_right_side(jax.random.fold_in(arg_keys[3], 71), 0),
        "faces": draw_faces(jax.random.fold_in(arg_keys[3], 71), 0),
        "widths": draw_widths(jax.random.fold_in(arg_keys[3], 71), 0),
    }


def solve_level(level_field, faces, widths):
    spectrum = jnp.fft.rfft(level_field, axis=1)
    wave_count = NX // 2 + 1
    wave_index = jnp.arange(wave_count).astype(jnp.float32)
    kappa_term = (3.0 - 2.0 * jnp.cos(wave_index * (2.0 * jnp.pi / NX))) / (ASPECT * ASPECT)
    upper_face = jnp.concatenate([faces[1:], jnp.zeros((1,), jnp.float32)])
    sub_coef = -jnp.concatenate([jnp.zeros((1,), jnp.float32), faces[1:]])
    sup_coef = -upper_face

    def forward_sweep(carry_state, row_data):
        ratio_prev, value_prev = carry_state
        sub_row, face_row, upper_row, width_row, sup_row, source_row = row_data
        diag_row = (face_row + upper_row) + width_row * kappa_term
        denominator = diag_row - sub_row * ratio_prev
        ratio_new = sup_row / denominator
        value_new = ((width_row / ASPECT) * source_row - sub_row * value_prev) / denominator
        return (ratio_new, value_new), (ratio_new, value_new)

    start_state = (jnp.zeros((wave_count,), jnp.float32),
                   jnp.zeros((wave_count,), spectrum.dtype))
    _, (ratios, values) = lax.scan(forward_sweep, start_state,
                                   (sub_coef, faces, upper_face, widths, sup_coef, spectrum))

    def backward_sweep(next_value, row_data):
        ratio_row, value_row = row_data
        current = value_row - ratio_row * next_value
        return current, current

    _, solved = lax.scan(backward_sweep, jnp.zeros_like(start_state[1]), (ratios, values), reverse=True)
    return jnp.fft.irfft(solved, n=NX, axis=1).astype(jnp.float32)


def reference(right_side, faces, widths):
    def one_level(level_field):
        return solve_level(level_field, faces, widths)

    return lax.map(one_level, right_side)
```

```python
import functools

import jax
import jax.numpy as jnp
import numpy as np
from jax import lax
from jax.experimental import pallas as pl
from jax.experimental.pallas import tpu as pltpu
from jax.sharding import PartitionSpec as P

MESH = pl.DeviceIdType.MESH
RADIX = 128
NX = RADIX * RADIX
NZ = 8
GROUPS = 32
BLOCKS = 16
ROWS = 64
HALF = 32
ASPECT = 128
F32 = jnp.float32
BF16 = jnp.bfloat16
GROUNDED = 1e30


def split_table(table):
    table = np.asarray(table, np.float32)
    high = table.astype(BF16)
    low = (table - high.astype(np.float32)).astype(BF16)
    return high, low


def tables():
    small = 2.0 * np.pi * (np.outer(np.arange(RADIX), np.arange(RADIX)) % RADIX) / RADIX
    cosine, sine = np.cos(small), np.sin(small)
    turn = 2.0 * np.pi * np.outer(np.arange(RADIX), np.arange(RADIX)) / NX
    forward = np.zeros((GROUPS, 2, 4, GROUPS, 2, 4))
    cos6 = cosine.reshape(GROUPS, 4, GROUPS, 4)
    sin6 = sine.reshape(GROUPS, 4, GROUPS, 4)
    forward[:, 0, :, :, 0, :] = cos6
    forward[:, 0, :, :, 1, :] = sin6
    forward[:, 1, :, :, 0, :] = -sin6
    forward[:, 1, :, :, 1, :] = cos6
    forward = forward.reshape(256, 256)
    right = np.concatenate([cosine, sine], axis=1)
    turn_cos = np.zeros((GROUPS, 2, 4, RADIX))
    turn_sin = np.zeros((GROUPS, 2, 4, RADIX))
    turn_cos[:, 0] = np.cos(turn).reshape(GROUPS, 4, RADIX)
    turn_cos[:, 1] = turn_cos[:, 0]
    turn_sin[:, 0] = np.sin(turn).reshape(GROUPS, 4, RADIX)
    turn_sin[:, 1] = -turn_sin[:, 0]
    left = np.stack(split_table(forward) + split_table(forward.T / NX))
    sides = np.stack(split_table(right))
    turns = np.stack([turn_cos.reshape(256, RADIX), turn_sin.reshape(256, RADIX)]).astype(np.float32)
    return left, sides, turns


def split_values(values):
    high = values.astype(BF16)
    low = (values - high.astype(F32)).astype(BF16)
    return high, low


def dot(a, b):
    return jnp.dot(a, b, preferred_element_type=F32)


def swap_parts(values):
    shape = values.shape
    tiles = values.reshape(shape[0] // 8, 8, shape[1])
    return pltpu.roll(tiles, 4, 1).reshape(shape)


def kernel(x, faces, widths, left_hbm, sides_hbm, turns_hbm, out,
           s1, r1, s2, r2, s3, r3, s4, r4, left, sides, turns,
           coef, coefs, ends, ends_all, join, phi, psi, part_r, part_u, part_v, cur_i, cur_j,
           in_sem, tab_sem, send_sem, recv_sem, csend, crecv, esend, erecv, out_sem):
    g = lax.axis_index("gx")
    r = lax.axis_index("gy")

    def line_peer(i):
        return (g + i) % GROUPS

    def block_peer(i):
        return (r + i) % BLOCKS

    barrier = pltpu.get_barrier_semaphore()

    def greet_line(i, carry):
        pl.semaphore_signal(barrier, inc=1, device_id=(line_peer(i), r), device_id_type=MESH)
        return carry

    def greet_block(i, carry):
        pl.semaphore_signal(barrier, inc=1, device_id=(g, block_peer(i)), device_id_type=MESH)
        return carry

    lax.fori_loop(1, GROUPS, greet_line, 0)
    lax.fori_loop(1, BLOCKS, greet_block, 0)

    for h in range(2):
        for level in range(2):
            for c in range(4):
                pltpu.make_async_copy(
                    x.at[level, pl.ds(HALF * h, HALF), pl.ds(128 * c, 128)],
                    s1.at[h, :, level * 4 + c, :], in_sem.at[h]).start()
    pltpu.make_async_copy(left_hbm, left, tab_sem.at[0]).start()
    pltpu.make_async_copy(sides_hbm, sides, tab_sem.at[1]).start()
    pltpu.make_async_copy(turns_hbm, turns, tab_sem.at[2]).start()

    sub = lax.broadcasted_iota(jnp.int32, (8, 128), 0)
    lane = lax.broadcasted_iota(jnp.int32, (8, 128), 1)
    wave = 4 * g + sub % 4 + RADIX * lane
    kappa = (3.0 - 2.0 * jnp.cos(wave.astype(F32) * (2.0 * np.pi / NX))) / float(ASPECT * ASPECT)
    sign = jnp.where(sub < 4, 1.0, -1.0).astype(F32)

    def grow(i, abc):
        a, b, c = abc
        f = faces[i]
        inverse = 1.0 / (b + c + f)
        pass_b = b * inverse
        return a + pass_b * c, pass_b * f, widths[i] * kappa + (c * inverse) * f

    zero = jnp.zeros((8, 128), F32)
    a, b, c = lax.fori_loop(1, ROWS, grow, (zero, zero + faces[0], widths[0] * kappa))
    coef[0] = a
    coef[1] = b
    coef[2] = c

    pl.semaphore_wait(barrier, GROUPS - 1 + BLOCKS - 1)

    def exchange(source, target, h, at):
        def send(i, carry):
            q = line_peer(i)
            pltpu.make_async_remote_copy(
                source.at[h, q], target.at[h, g], send_sem.at[at], recv_sem.at[at],
                device_id=(q, r), device_id_type=MESH).start()
            return carry

        lax.fori_loop(1, GROUPS, send, 0)
        pltpu.make_async_copy(source.at[h, g], target.at[h, g], recv_sem.at[at]).start()

    def arrived(target, h, at):
        pltpu.make_async_copy(target.at[h], target.at[h], recv_sem.at[at]).wait()

    for h in range(2):
        pltpu.make_async_copy(s1.at[h], s1.at[h], in_sem.at[h]).wait()
        exchange(s1, r1, h, h)

    def send_coef(i, carry):
        pltpu.make_async_remote_copy(
            coef, coefs.at[r], csend, crecv,
            device_id=(g, block_peer(i)), device_id_type=MESH).start()
        return carry

    lax.fori_loop(1, BLOCKS, send_coef, 0)

    pltpu.make_async_copy(left_hbm, left, tab_sem.at[0]).wait()
    pltpu.make_async_copy(sides_hbm, sides, tab_sem.at[1]).wait()
    pltpu.make_async_copy(turns_hbm, turns, tab_sem.at[2]).wait()

    def left_product(at, values):
        high, low = split_values(values)
        return dot(left[at], high) + (dot(left[at], low) + dot(left[at + 1], high))

    def right_product(values, direction):
        high, low = split_values(values)
        both = dot(high, sides[0]) + (dot(low, sides[0]) + dot(high, sides[1]))
        tiles = swap_parts(both[:, 128:]).reshape(GROUPS, 8, 128)
        return both[:, :128].reshape(GROUPS, 8, 128) + tiles * (sign * direction)

    for h in range(2):
        arrived(r1, h, h)
        first = left_product(0, r1[h].reshape(256, 128))
        turned = first * turns[0] + swap_parts(first) * turns[1]
        s2[h] = right_product(turned, 1.0)
        exchange(s2, r2, h, 2 + h)

    pltpu.make_async_copy(coefs.at[pl.ds(0, BLOCKS - 1)], coefs.at[pl.ds(0, BLOCKS - 1)], crecv).wait()

    def from_below(m, shunt):
        a, b, c = coefs[m, 0], coefs[m, 1], coefs[m, 2]
        share = b / (b + (shunt + a))
        join[m] = share
        return c + (shunt + a) * share

    def from_above(i, shunt):
        m = BLOCKS - 1 - i
        a, b, c = coefs[m, 0], coefs[m, 1], coefs[m, 2]
        share = b / (b + (shunt + c))
        join[m] = share
        return a + (shunt + c) * share

    below = lax.fori_loop(0, r, from_below, zero + GROUNDED)
    above = lax.fori_loop(0, BLOCKS - 1 - r, from_above, zero)

    def up(i, state):
        shunt, through = state
        f = faces[i]
        share = f / (f + shunt)
        shunt = widths[i] * kappa + shunt * share
        through = through * share
        phi[i] = share
        part_r[i] = shunt
        part_u[i] = through
        return shunt, through

    lax.fori_loop(0, ROWS, up, (below, zero + 1.0))

    def down(j, state):
        shunt, through = state
        i = ROWS - 1 - j
        f = faces[i]
        total = 1.0 / (part_r[i] + shunt)
        part_r[i] = total
        part_u[i] = part_u[i] * total
        part_v[i] = through * total
        inner = widths[i] * kappa + shunt
        share = f / (f + inner)
        psi[i] = share
        return inner * share, through * share

    lax.fori_loop(0, ROWS, down, (above, zero + 1.0))

    for h in range(2):
        arrived(r2, h, 2 + h)

    def sweep(it, state):
        going_up, going_down = state
        for u in range(8):
            i = it * 8 + u
            going_up = r2[i // HALF, i % HALF] * (widths[i] * (1.0 / ASPECT)) + phi[i] * going_up
            cur_i[i] = going_up
            j = ROWS - 1 - i
            cur_j[j] = going_down
            going_down = psi[j] * (r2[j // HALF, j % HALF] * (widths[j] * (1.0 / ASPECT)) + going_down)
        return going_up, going_down

    going_up, going_down = lax.fori_loop(0, ROWS // 8, sweep, (zero, zero))
    ends[0] = going_up
    ends[1] = going_down

    def send_end(i, carry):
        q = block_peer(i)
        pltpu.make_async_remote_copy(
            ends.at[jnp.where(q < r, 1, 0)], ends_all.at[r], esend, erecv,
            device_id=(g, q), device_id_type=MESH).start()
        return carry

    lax.fori_loop(1, BLOCKS, send_end, 0)

    def own(it, carry):
        for u in range(8):
            i = it * 8 + u
            cur_i[i] = (cur_i[i] + cur_j[i]) * part_r[i]
        return carry

    lax.fori_loop(0, ROWS // 8, own, 0)

    pltpu.make_async_copy(ends_all.at[pl.ds(0, BLOCKS - 1)], ends_all.at[pl.ds(0, BLOCKS - 1)], erecv).wait()

    def add_below(m, current):
        return ends_all[m] + join[m] * current

    def add_above(i, current):
        m = BLOCKS - 1 - i
        return ends_all[m] + join[m] * current

    current_below = lax.fori_loop(0, r, add_below, zero)
    current_above = lax.fori_loop(0, BLOCKS - 1 - r, add_above, zero)

    for h in range(2):
        def finish(it, carry):
            for u in range(8):
                i = it * 8 + u
                m = HALF * h + i
                s3[h, i] = cur_i[m] + part_u[m] * current_below + part_v[m] * current_above
            return carry

        lax.fori_loop(0, HALF // 8, finish, 0)
        exchange(s3, r3, h, 4 + h)

    for h in range(2):
        arrived(r3, h, 4 + h)
        back = right_product(r3[h].reshape(256, 128), -1.0).reshape(256, 128)
        turned = back * turns[0] - swap_parts(back) * turns[1]
        s4[h] = left_product(2, turned).reshape(GROUPS, 8, 128)
        exchange(s4, r4, h, 6 + h)

    for h in range(2):
        arrived(r4, h, 6 + h)
        for level in range(2):
            for c in range(4):
                pltpu.make_async_copy(
                    r4.at[h, :, level * 4 + c, :],
                    out.at[level, pl.ds(HALF * h, HALF), pl.ds(128 * c, 128)], out_sem.at[h]).start()

    sent = (s1, s2, s3, s4)
    for n in range(4):
        for h in range(2):
            block = sent[n].at[h, pl.ds(0, GROUPS - 1)]
            pltpu.make_async_copy(block, block, send_sem.at[2 * n + h]).wait()
    pltpu.make_async_copy(coefs.at[pl.ds(0, BLOCKS - 1)], coefs.at[pl.ds(0, BLOCKS - 1)], csend).wait()
    pltpu.make_async_copy(ends_all.at[pl.ds(0, BLOCKS - 1)], ends_all.at[pl.ds(0, BLOCKS - 1)], esend).wait()
    for h in range(2):
        pltpu.make_async_copy(r4.at[h], r4.at[h], out_sem.at[h]).wait()


def local(right_side, faces, widths):
    left, sides, turns = tables()
    any_space = pl.BlockSpec(memory_space=pl.ANY)
    scalars = pl.BlockSpec(memory_space=pltpu.SMEM)
    moved = pltpu.VMEM((2, GROUPS, 8, 128), F32)
    rows = pltpu.VMEM((ROWS, 8, 128), F32)
    dma = pltpu.SemaphoreType.DMA
    return pl.pallas_call(
        kernel,
        out_shape=jax.ShapeDtypeStruct((2, ROWS, 512), F32),
        in_specs=[any_space, scalars, scalars, any_space, any_space, any_space],
        out_specs=any_space,
        scratch_shapes=[moved] * 8 + [
            pltpu.VMEM((4, 256, 256), BF16),
            pltpu.VMEM((2, 128, 256), BF16),
            pltpu.VMEM((2, 256, 128), F32),
            pltpu.VMEM((3, 8, 128), F32),
            pltpu.VMEM((BLOCKS, 3, 8, 128), F32),
            pltpu.VMEM((2, 8, 128), F32),
            pltpu.VMEM((BLOCKS, 8, 128), F32),
            pltpu.VMEM((BLOCKS, 8, 128), F32),
        ] + [rows] * 7 + [
            dma((2,)), dma((3,)), dma((8,)), dma((8,)), dma, dma, dma, dma, dma((2,)),
        ],
        compiler_params=pltpu.CompilerParams(collective_id=0, has_side_effects=True),
    )(right_side, faces, widths, left, sides, turns)


def solution(mesh):
    spec = P(None, "gy", "gx")
    return jax.shard_map(local, mesh=mesh, in_specs=(spec, P("gy"), P("gy")), out_specs=spec, check_vma=False)
```

```python
import functools

import jax
import jax.numpy as jnp
import numpy as np
from jax import lax
from jax.experimental import pallas as pl
from jax.experimental.pallas import tpu as pltpu
from jax.sharding import PartitionSpec as P

MESH = pl.DeviceIdType.MESH
RADIX = 128
NX = RADIX * RADIX
NZ = 8
GROUPS = 32
BLOCKS = 16
ROWS = 64
HALF = 32
ASPECT = 128
F32 = jnp.float32
BF16 = jnp.bfloat16
GROUNDED = 1e30


def ring_distance(step, size):
    return min(step, size - step)


LINE_STEPS = sorted(
    [(dx, dz) for dx in range(4) for dz in range(NZ) if dx or dz],
    key=lambda s: (-ring_distance(s[0], 4), -ring_distance(s[1], NZ)))
BLOCK_STEPS = sorted(range(1, BLOCKS), key=lambda s: -ring_distance(s // 2, 8))


def split_table(table):
    table = np.asarray(table, np.float32)
    high = table.astype(BF16)
    low = (table - high.astype(np.float32)).astype(BF16)
    return high, low


def tables():
    small = 2.0 * np.pi * (np.outer(np.arange(RADIX), np.arange(RADIX)) % RADIX) / RADIX
    cosine, sine = np.cos(small), np.sin(small)
    turn = 2.0 * np.pi * np.outer(np.arange(RADIX), np.arange(RADIX)) / NX
    forward = np.zeros((GROUPS, 2, 4, GROUPS, 2, 4))
    cos6 = cosine.reshape(GROUPS, 4, GROUPS, 4)
    sin6 = sine.reshape(GROUPS, 4, GROUPS, 4)
    forward[:, 0, :, :, 0, :] = cos6
    forward[:, 0, :, :, 1, :] = sin6
    forward[:, 1, :, :, 0, :] = -sin6
    forward[:, 1, :, :, 1, :] = cos6
    forward = forward.reshape(256, 256)
    right = np.concatenate([cosine, sine], axis=1)
    turn_cos = np.zeros((GROUPS, 2, 4, RADIX))
    turn_sin = np.zeros((GROUPS, 2, 4, RADIX))
    turn_cos[:, 0] = np.cos(turn).reshape(GROUPS, 4, RADIX)
    turn_cos[:, 1] = turn_cos[:, 0]
    turn_sin[:, 0] = np.sin(turn).reshape(GROUPS, 4, RADIX)
    turn_sin[:, 1] = -turn_sin[:, 0]
    left = np.stack(split_table(forward) + split_table(forward.T / NX))
    sides = np.stack(split_table(right))
    turns = np.stack([turn_cos.reshape(256, RADIX), turn_sin.reshape(256, RADIX)]).astype(np.float32)
    return left, sides, turns


def split_values(values):
    high = values.astype(BF16)
    low = (values - high.astype(F32)).astype(BF16)
    return high, low


def dot(a, b):
    return jnp.dot(a, b, preferred_element_type=F32)


def swap_parts(values):
    shape = values.shape
    tiles = values.reshape(shape[0] // 8, 8, shape[1])
    return pltpu.roll(tiles, 4, 1).reshape(shape)


def kernel(x, faces_hbm, widths_hbm, left_hbm, sides_hbm, turns_hbm, r4,
           s1, r1, s2, r2, s3, r3, s4, left, sides, turns, faces, widths,
           coef, coefs, ends, ends_all, join, phi, psi, part_r, part_u, part_v, sum_up, sum_down, cur_i, cur_j,
           in_sem, tab_sem, send_sem, recv_sem, csend, crecv, esend, erecv):
    g = lax.axis_index("gx")
    r = lax.axis_index("gy")
    along_x = [((g // NZ + d) % 4) * NZ for d in range(4)]
    along_z = [(g % NZ + d) % NZ for d in range(NZ)]
    line_peers = [along_x[dx] + along_z[dz] for dx, dz in LINE_STEPS]
    block_peers = [(r // 2 * 2 + d // 2 * 2 + (r + d) % 2) % BLOCKS for d in BLOCK_STEPS]

    barrier = pltpu.get_barrier_semaphore()
    for q in line_peers:
        pl.semaphore_signal(barrier, inc=1, device_id=(q, r), device_id_type=MESH)
    for q in block_peers:
        pl.semaphore_signal(barrier, inc=1, device_id=(g, q), device_id_type=MESH)

    pltpu.make_async_copy(faces_hbm, faces, tab_sem.at[3]).start()
    pltpu.make_async_copy(widths_hbm, widths, tab_sem.at[4]).start()
    for h in range(2):
        for level in range(2):
            for c in range(4):
                pltpu.make_async_copy(
                    x.at[level, pl.ds(HALF * h, HALF), pl.ds(128 * c, 128)],
                    s1.at[h, :, level * 4 + c, :], in_sem.at[h]).start()
    pltpu.make_async_copy(left_hbm, left, tab_sem.at[0]).start()
    pltpu.make_async_copy(sides_hbm, sides, tab_sem.at[1]).start()
    pltpu.make_async_copy(turns_hbm, turns, tab_sem.at[2]).start()

    sub = lax.broadcasted_iota(jnp.int32, (8, 128), 0)
    lane = lax.broadcasted_iota(jnp.int32, (8, 128), 1)
    wave = 4 * g + sub % 4 + RADIX * lane
    kappa = (3.0 - 2.0 * jnp.cos(wave.astype(F32) * (2.0 * np.pi / NX))) / float(ASPECT * ASPECT)
    sign = jnp.where(sub < 4, 1.0, -1.0).astype(F32)

    pltpu.make_async_copy(faces_hbm, faces, tab_sem.at[3]).wait()
    pltpu.make_async_copy(widths_hbm, widths, tab_sem.at[4]).wait()

    def grow(i, abc):
        a, b, c = abc
        f = faces[i]
        inverse = 1.0 / (b + c + f)
        pass_b = b * inverse
        return a + pass_b * c, pass_b * f, widths[i] * kappa + (c * inverse) * f

    zero = jnp.zeros((8, 128), F32)
    a, b, c = lax.fori_loop(1, ROWS, grow, (zero, zero + faces[0], widths[0] * kappa))
    coef[0] = a
    coef[1] = b
    coef[2] = c

    pl.semaphore_wait(barrier, GROUPS - 1 + BLOCKS - 1)

    def exchange(source, target, h, at):
        for q in line_peers:
            pltpu.make_async_remote_copy(
                source.at[h, q], target.at[h, g], send_sem.at[at], recv_sem.at[at],
                device_id=(q, r), device_id_type=MESH).start()
        pltpu.make_async_copy(source.at[h, g], target.at[h, g], recv_sem.at[at]).start()

    def arrived(target, h, at):
        pltpu.make_async_copy(target.at[h], target.at[h], recv_sem.at[at]).wait()

    for h in range(2):
        pltpu.make_async_copy(s1.at[h], s1.at[h], in_sem.at[h]).wait()
        exchange(s1, r1, h, h)

    for q in block_peers:
        pltpu.make_async_remote_copy(
            coef, coefs.at[r], csend, crecv,
            device_id=(g, q), device_id_type=MESH).start()

    pltpu.make_async_copy(left_hbm, left, tab_sem.at[0]).wait()
    pltpu.make_async_copy(sides_hbm, sides, tab_sem.at[1]).wait()
    pltpu.make_async_copy(turns_hbm, turns, tab_sem.at[2]).wait()

    def left_product(at, values):
        high, low = split_values(values)
        return dot(left[at], high) + (dot(left[at], low) + dot(left[at + 1], high))

    def right_product(values, direction):
        high, low = split_values(values)
        both = dot(high, sides[0]) + (dot(low, sides[0]) + dot(high, sides[1]))
        tiles = swap_parts(both[:, 128:]).reshape(GROUPS, 8, 128)
        return both[:, :128].reshape(GROUPS, 8, 128) + tiles * (sign * direction)

    for h in range(2):
        arrived(r1, h, h)
        first = left_product(0, r1[h].reshape(256, 128))
        turned = first * turns[0] + swap_parts(first) * turns[1]
        s2[h] = right_product(turned, 1.0)
        exchange(s2, r2, h, 2 + h)

    pltpu.make_async_copy(coefs.at[pl.ds(0, BLOCKS - 1)], coefs.at[pl.ds(0, BLOCKS - 1)], crecv).wait()

    def from_below(m, shunt):
        a, b, c = coefs[m, 0], coefs[m, 1], coefs[m, 2]
        share = b / (b + (shunt + a))
        join[m] = share
        return c + (shunt + a) * share

    def from_above(i, shunt):
        m = BLOCKS - 1 - i
        a, b, c = coefs[m, 0], coefs[m, 1], coefs[m, 2]
        share = b / (b + (shunt + c))
        join[m] = share
        return a + (shunt + c) * share

    below = lax.fori_loop(0, r, from_below, zero + GROUNDED)
    above = lax.fori_loop(0, BLOCKS - 1 - r, from_above, zero)

    def up(i, state):
        shunt, through = state
        f = faces[i]
        share = f / (f + shunt)
        shunt = widths[i] * kappa + shunt * share
        through = through * share
        phi[i] = share
        part_r[i] = shunt
        part_u[i] = through
        return shunt, through

    lax.fori_loop(0, ROWS, up, (below, zero + 1.0))

    def down(j, state):
        shunt, through, passed = state
        i = ROWS - 1 - j
        f = faces[i]
        total = 1.0 / (part_r[i] + shunt)
        part_r[i] = total
        part_u[i] = part_u[i] * total
        part_v[i] = through * total
        inner = widths[i] * kappa + shunt
        share = f / (f + inner)
        psi[i] = share
        sum_up[i] = passed * (widths[i] * (1.0 / ASPECT))
        return inner * share, through * share, passed * phi[i]

    lax.fori_loop(0, ROWS, down, (above, zero + 1.0, zero + 1.0))

    def weigh(i, passed):
        passed = passed * psi[i]
        sum_down[i] = passed * (widths[i] * (1.0 / ASPECT))
        return passed

    lax.fori_loop(0, ROWS, weigh, zero + 1.0)

    into_last = [zero] * 4
    into_first = [zero] * 4
    for h in range(2):
        arrived(r2, h, 2 + h)
        for i in range(HALF):
            value = r2[h, i]
            into_last[i % 4] = into_last[i % 4] + value * sum_up[HALF * h + i]
            into_first[i % 4] = into_first[i % 4] + value * sum_down[HALF * h + i]
    ends[0] = (into_last[0] + into_last[1]) + (into_last[2] + into_last[3])
    ends[1] = (into_first[0] + into_first[1]) + (into_first[2] + into_first[3])

    for q in block_peers:
        pltpu.make_async_remote_copy(
            ends.at[jnp.where(q < r, 1, 0)], ends_all.at[r], esend, erecv,
            device_id=(g, q), device_id_type=MESH).start()

    def sweep(it, state):
        going_up, going_down = state
        for u in range(8):
            i = it * 8 + u
            going_up = r2[i // HALF, i % HALF] * (widths[i] * (1.0 / ASPECT)) + phi[i] * going_up
            cur_i[i] = going_up
            j = ROWS - 1 - i
            cur_j[j] = going_down
            going_down = psi[j] * (r2[j // HALF, j % HALF] * (widths[j] * (1.0 / ASPECT)) + going_down)
        return going_up, going_down

    lax.fori_loop(0, ROWS // 8, sweep, (zero, zero))

    def own(it, carry):
        for u in range(8):
            i = it * 8 + u
            cur_i[i] = (cur_i[i] + cur_j[i]) * part_r[i]
        return carry

    lax.fori_loop(0, ROWS // 8, own, 0)

    pltpu.make_async_copy(ends_all.at[pl.ds(0, BLOCKS - 1)], ends_all.at[pl.ds(0, BLOCKS - 1)], erecv).wait()

    def add_below(m, current):
        return ends_all[m] + join[m] * current

    def add_above(i, current):
        m = BLOCKS - 1 - i
        return ends_all[m] + join[m] * current

    current_below = lax.fori_loop(0, r, add_below, zero)
    current_above = lax.fori_loop(0, BLOCKS - 1 - r, add_above, zero)

    for h in range(2):
        def finish(it, carry):
            for u in range(8):
                i = it * 8 + u
                m = HALF * h + i
                s3[h, i] = cur_i[m] + part_u[m] * current_below + part_v[m] * current_above
            return carry

        lax.fori_loop(0, HALF // 8, finish, 0)
        exchange(s3, r3, h, 4 + h)

    for h in range(2):
        arrived(r3, h, 4 + h)
        back = right_product(r3[h].reshape(256, 128), -1.0).reshape(256, 128)
        turned = back * turns[0] - swap_parts(back) * turns[1]
        s4[h] = left_product(2, turned).reshape(GROUPS, 8, 128)
        exchange(s4, r4, h, 6 + h)

    for h in range(2):
        arrived(r4, h, 6 + h)

    sent = (s1, s2, s3, s4)
    for n in range(4):
        for h in range(2):
            block = sent[n].at[h, pl.ds(0, GROUPS - 1)]
            pltpu.make_async_copy(block, block, send_sem.at[2 * n + h]).wait()
    pltpu.make_async_copy(coefs.at[pl.ds(0, BLOCKS - 1)], coefs.at[pl.ds(0, BLOCKS - 1)], csend).wait()
    pltpu.make_async_copy(ends_all.at[pl.ds(0, BLOCKS - 1)], ends_all.at[pl.ds(0, BLOCKS - 1)], esend).wait()

def unpack(r4, out, sem):
    for h in range(2):
        for level in range(2):
            for c in range(4):
                pltpu.make_async_copy(
                    r4.at[h, :, level * 4 + c, :],
                    out.at[level, pl.ds(HALF * h, HALF), pl.ds(128 * c, 128)], sem).start()
    pltpu.make_async_copy(r4, r4, sem).wait()


def local(right_side, faces, widths):
    left, sides, turns = tables()
    any_space = pl.BlockSpec(memory_space=pl.ANY)
    moved = pltpu.VMEM((2, GROUPS, 8, 128), F32)
    rows = pltpu.VMEM((ROWS, 8, 128), F32)
    dma = pltpu.SemaphoreType.DMA
    moved_back = pl.pallas_call(
        kernel,
        out_shape=jax.ShapeDtypeStruct((2, GROUPS, 8, 128), F32),
        in_specs=[pl.BlockSpec(memory_space=pltpu.HBM)] * 6,
        out_specs=any_space,
        scratch_shapes=[moved] * 7 + [
            pltpu.VMEM((4, 256, 256), BF16),
            pltpu.VMEM((2, 128, 256), BF16),
            pltpu.VMEM((2, 256, 128), F32),
            pltpu.SMEM((ROWS,), F32),
            pltpu.SMEM((ROWS,), F32),
            pltpu.VMEM((3, 8, 128), F32),
            pltpu.VMEM((BLOCKS, 3, 8, 128), F32),
            pltpu.VMEM((2, 8, 128), F32),
            pltpu.VMEM((BLOCKS, 8, 128), F32),
            pltpu.VMEM((BLOCKS, 8, 128), F32),
        ] + [rows] * 9 + [
            dma((2,)), dma((5,)), dma((8,)), dma((8,)), dma, dma, dma, dma,
        ],
        compiler_params=pltpu.CompilerParams(
            collective_id=0, has_side_effects=True, vmem_limit_bytes=12 * 1024 * 1024),
    )(*[pltpu.with_memory_space_constraint(a, pltpu.HBM) for a in (right_side, faces, widths, left, sides, turns)])
    return pl.pallas_call(
        unpack,
        out_shape=jax.ShapeDtypeStruct((2, ROWS, 512), F32),
        in_specs=[any_space],
        out_specs=any_space,
        scratch_shapes=[dma],
        compiler_params=pltpu.CompilerParams(vmem_limit_bytes=1024 * 1024),
    )(moved_back)


def solution(mesh):
    spec = P(None, "gy", "gx")
    return jax.shard_map(local, mesh=mesh, in_specs=(spec, P("gy"), P("gy")), out_specs=spec, check_vma=False)
```

```python
import functools

import jax
import jax.numpy as jnp
import numpy as np
from jax import lax
from jax.experimental import pallas as pl
from jax.experimental.pallas import tpu as pltpu
from jax.sharding import PartitionSpec as P

MESH = pl.DeviceIdType.MESH
RADIX = 128
NX = RADIX * RADIX
NZ = 8
GROUPS = 32
BLOCKS = 16
ROWS = 64
HALF = 32
ASPECT = 128
F32 = jnp.float32
BF16 = jnp.bfloat16
GROUNDED = 1e30


def ring_distance(step, size):
    return min(step, size - step)


LINE_STEPS = sorted(
    [(dx, dz) for dx in range(4) for dz in range(NZ) if dx or dz],
    key=lambda s: -(1.9 * ring_distance(s[0], 4) + ring_distance(s[1], NZ)))
BLOCK_STEPS = sorted(range(1, BLOCKS), key=lambda s: -ring_distance(s // 2, 8))


def split_table(table):
    table = np.asarray(table, np.float32)
    high = table.astype(BF16)
    low = (table - high.astype(np.float32)).astype(BF16)
    return high, low


def tables():
    small = 2.0 * np.pi * (np.outer(np.arange(RADIX), np.arange(RADIX)) % RADIX) / RADIX
    cosine, sine = np.cos(small), np.sin(small)
    turn = 2.0 * np.pi * np.outer(np.arange(RADIX), np.arange(RADIX)) / NX
    forward = np.zeros((GROUPS, 2, 4, GROUPS, 2, 4))
    cos6 = cosine.reshape(GROUPS, 4, GROUPS, 4)
    sin6 = sine.reshape(GROUPS, 4, GROUPS, 4)
    forward[:, 0, :, :, 0, :] = cos6
    forward[:, 0, :, :, 1, :] = sin6
    forward[:, 1, :, :, 0, :] = -sin6
    forward[:, 1, :, :, 1, :] = cos6
    forward = forward.reshape(256, 256)
    right = np.concatenate([cosine, sine], axis=1)
    turn_cos = np.zeros((GROUPS, 2, 4, RADIX))
    turn_sin = np.zeros((GROUPS, 2, 4, RADIX))
    turn_cos[:, 0] = np.cos(turn).reshape(GROUPS, 4, RADIX)
    turn_cos[:, 1] = turn_cos[:, 0]
    turn_sin[:, 0] = np.sin(turn).reshape(GROUPS, 4, RADIX)
    turn_sin[:, 1] = -turn_sin[:, 0]
    left = []
    for table in (forward, forward.T / NX):
        high, low = split_table(table)
        left.append(np.concatenate([high, high, low], axis=1))
    left = np.stack(left)
    high, low = split_table(right)
    sides = np.concatenate([high, high, low], axis=0)
    turns = np.stack([turn_cos.reshape(256, RADIX), turn_sin.reshape(256, RADIX)]).astype(np.float32)
    return left, sides, turns


def split_values(values):
    high = values.astype(BF16)
    low = (values - high.astype(F32)).astype(BF16)
    return high, low


def dot(a, b):
    return jnp.dot(a, b, preferred_element_type=F32)


def swap_parts(values):
    shape = values.shape
    tiles = values.reshape(shape[0] // 8, 8, shape[1])
    return pltpu.roll(tiles, 4, 1).reshape(shape)


def kernel(x, faces_hbm, widths_hbm, left_hbm, sides_hbm, turns_hbm, out,
           s1, r1, s2, r2, s3, r3, s4, r4, left, sides, turns, faces, widths,
           coef, coefs, ends, ends_all, join, gain_below, gain_above, phi, psi, part_r, part_u, part_v, sum_up, sum_down, cur_i, cur_j,
           in_sem, tab_sem, send_sem, recv_sem, csend, crecv, esend, erecv):
    g = lax.axis_index("gx")
    r = lax.axis_index("gy")
    barrier = pltpu.get_barrier_semaphore()

    def farthest_first(i, size):
        return (size // 2 + (i + 1) // 2 * (1 - 2 * (i % 2))) % size

    def greet_line(i, carry):
        q = (g // NZ + farthest_first(i // NZ, 4)) % 4 * NZ + (g % NZ + farthest_first(i % NZ, NZ)) % NZ
        pl.semaphore_signal(barrier, inc=1, device_id=(q, r), device_id_type=MESH)
        return carry

    def greet_block(i, carry):
        pl.semaphore_signal(barrier, inc=1, device_id=(g, (r + i) % BLOCKS), device_id_type=MESH)
        return carry

    lax.fori_loop(0, GROUPS - 1, greet_line, 0)
    lax.fori_loop(1, BLOCKS, greet_block, 0)

    along_x = [((g // NZ + d) % 4) * NZ for d in range(4)]
    along_z = [(g % NZ + d) % NZ for d in range(NZ)]
    line_peers = [along_x[dx] + along_z[dz] for dx, dz in LINE_STEPS]
    block_peers = [(r // 2 * 2 + d // 2 * 2 + (r + d) % 2) % BLOCKS for d in BLOCK_STEPS]

    pltpu.make_async_copy(faces_hbm, faces, tab_sem.at[3]).start()
    pltpu.make_async_copy(widths_hbm, widths, tab_sem.at[4]).start()
    for h in range(2):
        for level in range(2):
            for c in range(4):
                pltpu.make_async_copy(
                    x.at[level, pl.ds(HALF * h, HALF), pl.ds(128 * c, 128)],
                    s1.at[h, :, level * 4 + c, :], in_sem.at[h]).start()
    pltpu.make_async_copy(left_hbm, left, tab_sem.at[0]).start()
    pltpu.make_async_copy(sides_hbm, sides, tab_sem.at[1]).start()
    pltpu.make_async_copy(turns_hbm, turns, tab_sem.at[2]).start()

    sub = lax.broadcasted_iota(jnp.int32, (8, 128), 0)
    lane = lax.broadcasted_iota(jnp.int32, (8, 128), 1)
    wave = 4 * g + sub % 4 + RADIX * lane
    kappa = (3.0 - 2.0 * jnp.cos(wave.astype(F32) * (2.0 * np.pi / NX))) / float(ASPECT * ASPECT)
    sign = jnp.where(sub < 4, 1.0, -1.0).astype(F32)

    pltpu.make_async_copy(faces_hbm, faces, tab_sem.at[3]).wait()
    pltpu.make_async_copy(widths_hbm, widths, tab_sem.at[4]).wait()

    def grow(i, abc):
        a, b, c = abc
        f = faces[i]
        inverse = 1.0 / (b + c + f)
        pass_b = b * inverse
        return a + pass_b * c, pass_b * f, widths[i] * kappa + (c * inverse) * f

    zero = jnp.zeros((8, 128), F32)
    a, b, c = lax.fori_loop(1, ROWS, grow, (zero, zero + faces[0], widths[0] * kappa))
    coef[0] = a
    coef[1] = b
    coef[2] = c

    pl.semaphore_wait(barrier, GROUPS - 1 + BLOCKS - 1)

    def exchange(source, target, h, at):
        for q in line_peers:
            pltpu.make_async_remote_copy(
                source.at[h, q], target.at[h, g], send_sem.at[at], recv_sem.at[at],
                device_id=(q, r), device_id_type=MESH).start()
        pltpu.make_async_copy(source.at[h, g], target.at[h, g], recv_sem.at[at]).start()

    def arrived(target, h, at):
        pltpu.make_async_copy(target.at[h], target.at[h], recv_sem.at[at]).wait()

    for h in range(2):
        pltpu.make_async_copy(s1.at[h], s1.at[h], in_sem.at[h]).wait()
        exchange(s1, r1, h, h)

    for q in block_peers:
        pltpu.make_async_remote_copy(
            coef, coefs.at[r], csend, crecv,
            device_id=(g, q), device_id_type=MESH).start()

    pltpu.make_async_copy(left_hbm, left, tab_sem.at[0]).wait()
    pltpu.make_async_copy(sides_hbm, sides, tab_sem.at[1]).wait()
    pltpu.make_async_copy(turns_hbm, turns, tab_sem.at[2]).wait()

    def left_product(at, values):
        high, low = split_values(values)
        return dot(left[at], jnp.concatenate([high, low, high], axis=0))

    def right_product(values, direction):
        high, low = split_values(values)
        both = dot(jnp.concatenate([high, low, high], axis=1), sides[...])
        tiles = swap_parts(both[:, 128:]).reshape(GROUPS, 8, 128)
        return both[:, :128].reshape(GROUPS, 8, 128) + tiles * (sign * direction)

    for h in range(2):
        arrived(r1, h, h)
        first = left_product(0, r1[h].reshape(256, 128))
        turned = first * turns[0] + swap_parts(first) * turns[1]
        s2[h] = right_product(turned, 1.0)
        exchange(s2, r2, h, 2 + h)

    pltpu.make_async_copy(coefs.at[pl.ds(0, BLOCKS - 1)], coefs.at[pl.ds(0, BLOCKS - 1)], crecv).wait()

    def from_below(m, shunt):
        a, b, c = coefs[m, 0], coefs[m, 1], coefs[m, 2]
        share = b / (b + (shunt + a))
        join[m] = share
        return c + (shunt + a) * share

    def from_above(i, shunt):
        m = BLOCKS - 1 - i
        a, b, c = coefs[m, 0], coefs[m, 1], coefs[m, 2]
        share = b / (b + (shunt + c))
        join[m] = share
        return a + (shunt + c) * share

    below = lax.fori_loop(0, r, from_below, zero + GROUNDED)
    above = lax.fori_loop(0, BLOCKS - 1 - r, from_above, zero)

    for m in range(BLOCKS):
        gain_below[m] = zero
        gain_above[m] = zero
    ends_all[r] = zero

    def reach_below(i, gain):
        m = r - 1 - i
        gain_below[m] = gain
        return gain * join[m]

    def reach_above(i, gain):
        m = r + 1 + i
        gain_above[m] = gain
        return gain * join[m]

    lax.fori_loop(0, r, reach_below, zero + 1.0)
    lax.fori_loop(0, BLOCKS - 1 - r, reach_above, zero + 1.0)

    def up(i, state):
        shunt, through = state
        f = faces[i]
        share = f / (f + shunt)
        shunt = widths[i] * kappa + shunt * share
        through = through * share
        phi[i] = share
        part_r[i] = shunt
        part_u[i] = through
        return shunt, through

    lax.fori_loop(0, ROWS, up, (below, zero + 1.0))

    def down(j, state):
        shunt, through, passed = state
        i = ROWS - 1 - j
        f = faces[i]
        total = 1.0 / (part_r[i] + shunt)
        part_r[i] = total
        part_u[i] = part_u[i] * total
        part_v[i] = through * total
        inner = widths[i] * kappa + shunt
        share = f / (f + inner)
        psi[i] = share
        sum_up[i] = passed * (widths[i] * (1.0 / ASPECT))
        return inner * share, through * share, passed * phi[i]

    lax.fori_loop(0, ROWS, down, (above, zero + 1.0, zero + 1.0))

    def weigh(i, passed):
        passed = passed * psi[i]
        sum_down[i] = passed * (widths[i] * (1.0 / ASPECT))
        return passed

    lax.fori_loop(0, ROWS, weigh, zero + 1.0)

    into_last = [zero] * 4
    into_first = [zero] * 4
    for h in range(2):
        arrived(r2, h, 2 + h)
        for i in range(HALF):
            value = r2[h, i]
            into_last[i % 4] = into_last[i % 4] + value * sum_up[HALF * h + i]
            into_first[i % 4] = into_first[i % 4] + value * sum_down[HALF * h + i]
    ends[0] = (into_last[0] + into_last[1]) + (into_last[2] + into_last[3])
    ends[1] = (into_first[0] + into_first[1]) + (into_first[2] + into_first[3])

    for q in block_peers:
        pltpu.make_async_remote_copy(
            ends.at[jnp.where(q < r, 1, 0)], ends_all.at[r], esend, erecv,
            device_id=(g, q), device_id_type=MESH).start()

    def sweep(it, state):
        going_up, going_down = state
        for u in range(8):
            i = it * 8 + u
            going_up = r2[i // HALF, i % HALF] * (widths[i] * (1.0 / ASPECT)) + phi[i] * going_up
            cur_i[i] = going_up
            j = ROWS - 1 - i
            cur_j[j] = going_down
            going_down = psi[j] * (r2[j // HALF, j % HALF] * (widths[j] * (1.0 / ASPECT)) + going_down)
        return going_up, going_down

    lax.fori_loop(0, ROWS // 8, sweep, (zero, zero))

    def own(it, carry):
        for u in range(8):
            i = it * 8 + u
            cur_i[i] = (cur_i[i] + cur_j[i]) * part_r[i]
        return carry

    lax.fori_loop(0, ROWS // 8, own, 0)

    pltpu.make_async_copy(ends_all.at[pl.ds(0, BLOCKS - 1)], ends_all.at[pl.ds(0, BLOCKS - 1)], erecv).wait()

    def total(gains):
        terms = [ends_all[m] * gains[m] for m in range(BLOCKS)]
        while len(terms) > 1:
            terms = [terms[m] + terms[m + 1] for m in range(0, len(terms), 2)]
        return terms[0]

    current_below = total(gain_below)
    current_above = total(gain_above)

    for h in range(2):
        def finish(it, carry):
            for u in range(8):
                i = it * 8 + u
                m = HALF * h + i
                s3[h, i] = cur_i[m] + part_u[m] * current_below + part_v[m] * current_above
            return carry

        lax.fori_loop(0, HALF // 8, finish, 0)
        exchange(s3, r3, h, 4 + h)

    for h in range(2):
        arrived(r3, h, 4 + h)
        back = right_product(r3[h].reshape(256, 128), -1.0).reshape(256, 128)
        turned = back * turns[0] - swap_parts(back) * turns[1]
        s4[h] = left_product(1, turned).reshape(GROUPS, 8, 128)
        exchange(s4, r4, h, 6 + h)

    for h in range(2):
        arrived(r4, h, 6 + h)
        for level in range(2):
            for c in range(4):
                for t in range(0, HALF, 8):
                    out[level, pl.ds(HALF * h + t, 8), pl.ds(128 * c, 128)] = r4[h, pl.ds(t, 8), level * 4 + c, :]

    sent = (s1, s2, s3, s4)
    for n in range(4):
        for h in range(2):
            block = sent[n].at[h, pl.ds(0, GROUPS - 1)]
            pltpu.make_async_copy(block, block, send_sem.at[2 * n + h]).wait()
    pltpu.make_async_copy(coefs.at[pl.ds(0, BLOCKS - 1)], coefs.at[pl.ds(0, BLOCKS - 1)], csend).wait()
    pltpu.make_async_copy(ends_all.at[pl.ds(0, BLOCKS - 1)], ends_all.at[pl.ds(0, BLOCKS - 1)], esend).wait()

def place(held, out, sem):
    for level in range(2):
        for t in range(0, ROWS, 16):
            pltpu.make_async_copy(held.at[level, pl.ds(t, 16)], out.at[level, pl.ds(t, 16)], sem).start()
    pltpu.make_async_copy(held, out, sem).wait()


def local(right_side, faces, widths):
    left, sides, turns = tables()
    any_space = pl.BlockSpec(memory_space=pl.ANY)
    moved = pltpu.VMEM((2, GROUPS, 8, 128), F32)
    rows = pltpu.VMEM((ROWS, 8, 128), F32)
    dma = pltpu.SemaphoreType.DMA
    held = pl.pallas_call(
        kernel,
        out_shape=jax.ShapeDtypeStruct((2, ROWS, 512), F32),
        in_specs=[pl.BlockSpec(memory_space=pltpu.HBM)] * 6,
        out_specs=pl.BlockSpec(memory_space=pltpu.VMEM),
        scratch_shapes=[moved] * 8 + [
            pltpu.VMEM((2, 256, 768), BF16),
            pltpu.VMEM((384, 256), BF16),
            pltpu.VMEM((2, 256, 128), F32),
            pltpu.SMEM((ROWS,), F32),
            pltpu.SMEM((ROWS,), F32),
            pltpu.VMEM((3, 8, 128), F32),
            pltpu.VMEM((BLOCKS, 3, 8, 128), F32),
            pltpu.VMEM((2, 8, 128), F32),
            pltpu.VMEM((BLOCKS, 8, 128), F32),
            pltpu.VMEM((BLOCKS, 8, 128), F32),
            pltpu.VMEM((BLOCKS, 8, 128), F32),
            pltpu.VMEM((BLOCKS, 8, 128), F32),
        ] + [rows] * 9 + [
            dma((2,)), dma((5,)), dma((8,)), dma((8,)), dma, dma, dma, dma,
        ],
        compiler_params=pltpu.CompilerParams(
            collective_id=0, has_side_effects=True, vmem_limit_bytes=12 * 1024 * 1024),
    )(*[pltpu.with_memory_space_constraint(a, pltpu.HBM) for a in (right_side, faces, widths, left, sides, turns)])
    return pl.pallas_call(
        place,
        out_shape=jax.ShapeDtypeStruct((2, ROWS, 512), F32),
        in_specs=[any_space],
        out_specs=any_space,
        scratch_shapes=[dma],
        compiler_params=pltpu.CompilerParams(vmem_limit_bytes=1024 * 1024),
    )(held)


def solution(mesh):
    spec = P(None, "gy", "gx")
    return jax.shard_map(local, mesh=mesh, in_specs=(spec, P("gy"), P("gy")), out_specs=spec, check_vma=False)
```

```python
import functools

import jax
import jax.numpy as jnp
import numpy as np
from jax import lax
from jax.experimental import pallas as pl
from jax.experimental.pallas import tpu as pltpu
from jax.sharding import PartitionSpec as P

MESH = pl.DeviceIdType.MESH
RADIX = 128
NX = RADIX * RADIX
NZ = 8
GROUPS = 32
BLOCKS = 16
ROWS = 64
HALF = 32
ASPECT = 128
F32 = jnp.float32
BF16 = jnp.bfloat16
GROUNDED = 1e30


def ring_distance(step, size):
    return min(step, size - step)


LINE_STEPS = sorted(
    [(dx, dz) for dx in range(4) for dz in range(NZ) if dx or dz],
    key=lambda s: -(1.9 * ring_distance(s[0], 4) + ring_distance(s[1], NZ)))
BLOCK_STEPS = sorted(range(1, BLOCKS), key=lambda s: -ring_distance(s // 2, 8))


def split_table(table):
    table = np.asarray(table, np.float32)
    high = table.astype(BF16)
    low = (table - high.astype(np.float32)).astype(BF16)
    return high, low


def tables():
    small = 2.0 * np.pi * (np.outer(np.arange(RADIX), np.arange(RADIX)) % RADIX) / RADIX
    cosine, sine = np.cos(small), np.sin(small)
    turn = 2.0 * np.pi * np.outer(np.arange(RADIX), np.arange(RADIX)) / NX
    forward = np.zeros((GROUPS, 2, 4, GROUPS, 2, 4))
    cos6 = cosine.reshape(GROUPS, 4, GROUPS, 4)
    sin6 = sine.reshape(GROUPS, 4, GROUPS, 4)
    forward[:, 0, :, :, 0, :] = cos6
    forward[:, 0, :, :, 1, :] = sin6
    forward[:, 1, :, :, 0, :] = -sin6
    forward[:, 1, :, :, 1, :] = cos6
    forward = forward.reshape(256, 256)
    right = np.concatenate([cosine, sine], axis=1)
    turn_cos = np.zeros((GROUPS, 2, 4, RADIX))
    turn_sin = np.zeros((GROUPS, 2, 4, RADIX))
    turn_cos[:, 0] = np.cos(turn).reshape(GROUPS, 4, RADIX)
    turn_cos[:, 1] = turn_cos[:, 0]
    turn_sin[:, 0] = np.sin(turn).reshape(GROUPS, 4, RADIX)
    turn_sin[:, 1] = -turn_sin[:, 0]
    left = []
    for table in (forward, forward.T / NX):
        high, low = split_table(table)
        left.append(np.concatenate([high, high, low], axis=1))
    left = np.stack(left)
    high, low = split_table(right)
    sides = np.concatenate([high, high, low], axis=0)
    turns = np.stack([turn_cos.reshape(256, RADIX), turn_sin.reshape(256, RADIX)]).astype(np.float32)
    return left, sides, turns


def split_values(values):
    high = values.astype(BF16)
    low = (values - high.astype(F32)).astype(BF16)
    return high, low


def dot(a, b):
    return jnp.dot(a, b, preferred_element_type=F32)


def swap_parts(values):
    shape = values.shape
    tiles = values.reshape(shape[0] // 8, 8, shape[1])
    return pltpu.roll(tiles, 4, 1).reshape(shape)


def kernel(x, faces_hbm, widths_hbm, left_hbm, sides_hbm, turns_hbm, out,
           s1, r1, s2, r2, s3, r3, s4, r4, left, sides, turns, faces, widths,
           coef, coefs, ends, ends_all, join, gain_below, gain_above, phi, psi, part_r, part_u, part_v, sum_up, sum_down, cur_i, cur_j,
           in_sem, tab_sem, send_sem, recv_sem, csend, crecv, esend, erecv):
    g = lax.axis_index("gx")
    r = lax.axis_index("gy")
    barrier = pltpu.get_barrier_semaphore()

    def farthest_first(i, size):
        return (size // 2 + (i + 1) // 2 * (1 - 2 * (i % 2))) % size

    def greet_line(i, carry):
        q = (g // NZ + farthest_first(i // NZ, 4)) % 4 * NZ + (g % NZ + farthest_first(i % NZ, NZ)) % NZ
        pl.semaphore_signal(barrier, inc=1, device_id=(q, r), device_id_type=MESH)
        return carry

    def greet_block(i, carry):
        pl.semaphore_signal(barrier, inc=1, device_id=(g, (r + i) % BLOCKS), device_id_type=MESH)
        return carry

    lax.fori_loop(0, GROUPS - 1, greet_line, 0)
    lax.fori_loop(1, BLOCKS, greet_block, 0)

    along_x = [((g // NZ + d) % 4) * NZ for d in range(4)]
    along_z = [(g % NZ + d) % NZ for d in range(NZ)]
    line_peers = [along_x[dx] + along_z[dz] for dx, dz in LINE_STEPS]
    block_peers = [(r // 2 * 2 + d // 2 * 2 + (r + d) % 2) % BLOCKS for d in BLOCK_STEPS]

    pltpu.make_async_copy(faces_hbm, faces, tab_sem.at[3]).start()
    pltpu.make_async_copy(widths_hbm, widths, tab_sem.at[4]).start()
    for h in range(2):
        for level in range(2):
            for c in range(4):
                pltpu.make_async_copy(
                    x.at[level, pl.ds(HALF * h, HALF), pl.ds(128 * c, 128)],
                    s1.at[h, :, level * 4 + c, :], in_sem.at[h]).start()
    pltpu.make_async_copy(left_hbm, left, tab_sem.at[0]).start()
    pltpu.make_async_copy(sides_hbm, sides, tab_sem.at[1]).start()
    pltpu.make_async_copy(turns_hbm, turns, tab_sem.at[2]).start()

    sub = lax.broadcasted_iota(jnp.int32, (8, 128), 0)
    lane = lax.broadcasted_iota(jnp.int32, (8, 128), 1)
    wave = 4 * g + sub % 4 + RADIX * lane
    kappa = (3.0 - 2.0 * jnp.cos(wave.astype(F32) * (2.0 * np.pi / NX))) / float(ASPECT * ASPECT)
    sign = jnp.where(sub < 4, 1.0, -1.0).astype(F32)

    pltpu.make_async_copy(faces_hbm, faces, tab_sem.at[3]).wait()
    pltpu.make_async_copy(widths_hbm, widths, tab_sem.at[4]).wait()

    def grow(i, abc):
        a, b, c = abc
        f = faces[i]
        inverse = 1.0 / (b + c + f)
        pass_b = b * inverse
        return a + pass_b * c, pass_b * f, widths[i] * kappa + (c * inverse) * f

    zero = jnp.zeros((8, 128), F32)
    a, b, c = lax.fori_loop(1, ROWS, grow, (zero, zero + faces[0], widths[0] * kappa))
    coef[0] = a
    coef[1] = b
    coef[2] = c

    pl.semaphore_wait(barrier, GROUPS - 1 + BLOCKS - 1)

    def exchange(source, target, h, at):
        for q in (line_peers[::-1] if at in (2, 6) else line_peers):
            pltpu.make_async_remote_copy(
                source.at[h, q], target.at[h, g], send_sem.at[at], recv_sem.at[at],
                device_id=(q, r), device_id_type=MESH).start()
        pltpu.make_async_copy(source.at[h, g], target.at[h, g], recv_sem.at[at]).start()

    def arrived(target, h, at):
        pltpu.make_async_copy(target.at[h], target.at[h], recv_sem.at[at]).wait()

    for h in range(2):
        pltpu.make_async_copy(s1.at[h], s1.at[h], in_sem.at[h]).wait()
        exchange(s1, r1, h, h)

    for q in block_peers:
        pltpu.make_async_remote_copy(
            coef, coefs.at[r], csend, crecv,
            device_id=(g, q), device_id_type=MESH).start()

    pltpu.make_async_copy(left_hbm, left, tab_sem.at[0]).wait()
    pltpu.make_async_copy(sides_hbm, sides, tab_sem.at[1]).wait()
    pltpu.make_async_copy(turns_hbm, turns, tab_sem.at[2]).wait()

    def left_product(at, values):
        high, low = split_values(values)
        return dot(left[at], jnp.concatenate([high, low, high], axis=0))

    def right_product(values, direction):
        high, low = split_values(values)
        both = dot(jnp.concatenate([high, low, high], axis=1), sides[...])
        tiles = swap_parts(both[:, 128:]).reshape(GROUPS, 8, 128)
        return both[:, :128].reshape(GROUPS, 8, 128) + tiles * (sign * direction)

    for h in range(2):
        arrived(r1, h, h)
        first = left_product(0, r1[h].reshape(256, 128))
        turned = first * turns[0] + swap_parts(first) * turns[1]
        s2[h] = right_product(turned, 1.0)
        exchange(s2, r2, h, 2 + h)

    pltpu.make_async_copy(coefs.at[pl.ds(0, BLOCKS - 1)], coefs.at[pl.ds(0, BLOCKS - 1)], crecv).wait()

    def from_below(m, shunt):
        a, b, c = coefs[m, 0], coefs[m, 1], coefs[m, 2]
        share = b / (b + (shunt + a))
        join[m] = share
        return c + (shunt + a) * share

    def from_above(i, shunt):
        m = BLOCKS - 1 - i
        a, b, c = coefs[m, 0], coefs[m, 1], coefs[m, 2]
        share = b / (b + (shunt + c))
        join[m] = share
        return a + (shunt + c) * share

    below = lax.fori_loop(0, r, from_below, zero + GROUNDED)
    above = lax.fori_loop(0, BLOCKS - 1 - r, from_above, zero)

    for m in range(BLOCKS):
        gain_below[m] = zero
        gain_above[m] = zero
    ends_all[r] = zero

    def reach_below(i, gain):
        m = r - 1 - i
        gain_below[m] = gain
        return gain * join[m]

    def reach_above(i, gain):
        m = r + 1 + i
        gain_above[m] = gain
        return gain * join[m]

    lax.fori_loop(0, r, reach_below, zero + 1.0)
    lax.fori_loop(0, BLOCKS - 1 - r, reach_above, zero + 1.0)

    def up(i, state):
        shunt, through = state
        f = faces[i]
        share = f / (f + shunt)
        shunt = widths[i] * kappa + shunt * share
        through = through * share
        phi[i] = share
        part_r[i] = shunt
        part_u[i] = through
        return shunt, through

    lax.fori_loop(0, ROWS, up, (below, zero + 1.0))

    def down(j, state):
        shunt, through, passed = state
        i = ROWS - 1 - j
        f = faces[i]
        total = 1.0 / (part_r[i] + shunt)
        part_r[i] = total
        part_u[i] = part_u[i] * total
        part_v[i] = through * total
        inner = widths[i] * kappa + shunt
        share = f / (f + inner)
        psi[i] = share
        sum_up[i] = passed * (widths[i] * (1.0 / ASPECT))
        return inner * share, through * share, passed * phi[i]

    lax.fori_loop(0, ROWS, down, (above, zero + 1.0, zero + 1.0))

    def weigh(i, passed):
        passed = passed * psi[i]
        sum_down[i] = passed * (widths[i] * (1.0 / ASPECT))
        return passed

    lax.fori_loop(0, ROWS, weigh, zero + 1.0)

    into_last = [zero] * 4
    into_first = [zero] * 4
    for h in range(2):
        arrived(r2, h, 2 + h)
        for i in range(HALF):
            value = r2[h, i]
            into_last[i % 4] = into_last[i % 4] + value * sum_up[HALF * h + i]
            into_first[i % 4] = into_first[i % 4] + value * sum_down[HALF * h + i]
    ends[0] = (into_last[0] + into_last[1]) + (into_last[2] + into_last[3])
    ends[1] = (into_first[0] + into_first[1]) + (into_first[2] + into_first[3])

    for q in block_peers:
        pltpu.make_async_remote_copy(
            ends.at[jnp.where(q < r, 1, 0)], ends_all.at[r], esend, erecv,
            device_id=(g, q), device_id_type=MESH).start()

    def sweep(it, state):
        going_up, going_down = state
        for u in range(8):
            i = it * 8 + u
            going_up = r2[i // HALF, i % HALF] * (widths[i] * (1.0 / ASPECT)) + phi[i] * going_up
            cur_i[i] = going_up
            j = ROWS - 1 - i
            cur_j[j] = going_down
            going_down = psi[j] * (r2[j // HALF, j % HALF] * (widths[j] * (1.0 / ASPECT)) + going_down)
        return going_up, going_down

    lax.fori_loop(0, ROWS // 8, sweep, (zero, zero))

    def own(it, carry):
        for u in range(8):
            i = it * 8 + u
            cur_i[i] = (cur_i[i] + cur_j[i]) * part_r[i]
        return carry

    lax.fori_loop(0, ROWS // 8, own, 0)

    pltpu.make_async_copy(ends_all.at[pl.ds(0, BLOCKS - 1)], ends_all.at[pl.ds(0, BLOCKS - 1)], erecv).wait()

    def total(gains):
        terms = [ends_all[m] * gains[m] for m in range(BLOCKS)]
        while len(terms) > 1:
            terms = [terms[m] + terms[m + 1] for m in range(0, len(terms), 2)]
        return terms[0]

    current_below = total(gain_below)
    current_above = total(gain_above)

    for h in range(2):
        def finish(it, carry):
            for u in range(8):
                i = it * 8 + u
                m = HALF * h + i
                s3[h, i] = cur_i[m] + part_u[m] * current_below + part_v[m] * current_above
            return carry

        lax.fori_loop(0, HALF // 8, finish, 0)
        exchange(s3, r3, h, 4 + h)

    for h in range(2):
        arrived(r3, h, 4 + h)
        back = right_product(r3[h].reshape(256, 128), -1.0).reshape(256, 128)
        turned = back * turns[0] - swap_parts(back) * turns[1]
        s4[h] = left_product(1, turned).reshape(GROUPS, 8, 128)
        exchange(s4, r4, h, 6 + h)

    for h in range(2):
        arrived(r4, h, 6 + h)
        for level in range(2):
            for c in range(4):
                for t in range(0, HALF, 8):
                    out[level, pl.ds(HALF * h + t, 8), pl.ds(128 * c, 128)] = r4[h, pl.ds(t, 8), level * 4 + c, :]

    sent = (s1, s2, s3, s4)
    for n in range(4):
        for h in range(2):
            block = sent[n].at[h, pl.ds(0, GROUPS - 1)]
            pltpu.make_async_copy(block, block, send_sem.at[2 * n + h]).wait()
    pltpu.make_async_copy(coefs.at[pl.ds(0, BLOCKS - 1)], coefs.at[pl.ds(0, BLOCKS - 1)], csend).wait()
    pltpu.make_async_copy(ends_all.at[pl.ds(0, BLOCKS - 1)], ends_all.at[pl.ds(0, BLOCKS - 1)], esend).wait()

def place(held, out, sem):
    for level in range(2):
        for t in range(0, ROWS, 16):
            pltpu.make_async_copy(held.at[level, pl.ds(t, 16)], out.at[level, pl.ds(t, 16)], sem).start()
    pltpu.make_async_copy(held, out, sem).wait()


def local(right_side, faces, widths):
    left, sides, turns = tables()
    any_space = pl.BlockSpec(memory_space=pl.ANY)
    moved = pltpu.VMEM((2, GROUPS, 8, 128), F32)
    rows = pltpu.VMEM((ROWS, 8, 128), F32)
    dma = pltpu.SemaphoreType.DMA
    held = pl.pallas_call(
        kernel,
        out_shape=jax.ShapeDtypeStruct((2, ROWS, 512), F32),
        in_specs=[pl.BlockSpec(memory_space=pltpu.HBM)] * 6,
        out_specs=pl.BlockSpec(memory_space=pltpu.VMEM),
        scratch_shapes=[moved] * 8 + [
            pltpu.VMEM((2, 256, 768), BF16),
            pltpu.VMEM((384, 256), BF16),
            pltpu.VMEM((2, 256, 128), F32),
            pltpu.SMEM((ROWS,), F32),
            pltpu.SMEM((ROWS,), F32),
            pltpu.VMEM((3, 8, 128), F32),
            pltpu.VMEM((BLOCKS, 3, 8, 128), F32),
            pltpu.VMEM((2, 8, 128), F32),
            pltpu.VMEM((BLOCKS, 8, 128), F32),
            pltpu.VMEM((BLOCKS, 8, 128), F32),
            pltpu.VMEM((BLOCKS, 8, 128), F32),
            pltpu.VMEM((BLOCKS, 8, 128), F32),
        ] + [rows] * 9 + [
            dma((2,)), dma((5,)), dma((8,)), dma((8,)), dma, dma, dma, dma,
        ],
        compiler_params=pltpu.CompilerParams(
            collective_id=0, has_side_effects=True, vmem_limit_bytes=12 * 1024 * 1024),
    )(*[pltpu.with_memory_space_constraint(a, pltpu.HBM) for a in (right_side, faces, widths, left, sides, turns)])
    return pl.pallas_call(
        place,
        out_shape=jax.ShapeDtypeStruct((2, ROWS, 512), F32),
        in_specs=[any_space],
        out_specs=any_space,
        scratch_shapes=[dma],
        compiler_params=pltpu.CompilerParams(vmem_limit_bytes=1024 * 1024),
    )(held)


def solution(mesh):
    spec = P(None, "gy", "gx")
    return jax.shard_map(local, mesh=mesh, in_specs=(spec, P("gy"), P("gy")), out_specs=spec, check_vma=False)
```
